32 devices in a mesh: groups: 2 (over y), bx: 4 (over z), by: 2 (over x), bz: 2 (over core).
Axes of the slice: x: 2, y: 2, z: 4, core: 2. Of those that a mesh axis runs over, the one named last changes fastest.
Arguments:
- slab: float32 [4, 512, 1024], P(('groups', 'bz'), 'bx', 'by'), parts along dimension 0, may hold values from -6 to 6
- plane_test: float32 [2, 256], P('bz'), may hold values from -4 to 4
- row_test: float32 [512, 256], P('bx'), may hold values from -0.25 to 0.25
- col_test: float32 [1024, 256], P('by'), may hold values from -0.1875 to 0.1875
- core_planes: float32 [512, 2], P('bz'), may hold values from -4 to 4
- core_rows: float32 [512, 512], P(None, 'bx'), may hold values from -0.25 to 0.25
- core_cols: float32 [512, 1024], P(None, 'by'), may hold values from -0.1875 to 0.1875
Outputs:
- plane_sketch: float32 [4, 256], P(('groups', 'bz')), parts along dimension 0
- row_sketch: float32 [1024, 256], P(('groups', 'bx'), ('by', 'bz')), parts along dimension 0
- col_sketch: float32 [2048, 256], P(('groups', 'by'), ('bx', 'bz')), parts along dimension 0
- core_sketch: float32 [1024, 512, 512], P(('groups', 'bz'), 'bx', 'by'), parts along dimension 0
The draws below stay inside these ranges and needn't reach their ends.
There are 2 independent parts, one for each index of `groups`. The reference program is written for one: setup_inputs(seed, part) draws one part's arguments, and reference() takes and returns one part's arrays. A program takes and returns all parts, laid end to end along the dimension named above; an argument that names none is the same for every part. Nothing has to cross between parts.
All inputs are finite; a program needn't handle non-finite values.
Results may differ from the reference program's by a relative error of at most 0.00011.
Values sent between devices are 32-bit elements; how exact they have to be, the bound alone decides.
A program may use at most 128 MiB of HBM per device.

```python
import jax
import jax.numpy as jnp
from jax import lax

S = 512
K = 256
P_SIZE = 2
NR = 512
NC = 1024


def shard_levels(own_key, dims, pieces, smallest, top_value):
    level = 1.0
    for position, shards_of in pieces:
        heights = jax.random.uniform(jax.random.fold_in(jax.random.fold_in(own_key, 6), position), (shards_of,), jnp.float32, smallest / len(pieces), top_value / len(pieces))
        level = level * jnp.repeat(jnp.exp(heights), dims[position] // shards_of).reshape((-1,) + (1,) * (len(dims) - 1 - position))
    return level


def centred(rng, dims, spread, most, pieces=(), held_as=jnp.bfloat16):
    array = spread * jax.random.normal(rng, dims, jnp.float32)
    if pieces:
        array = array * shard_levels(rng, dims, pieces, -0.22, 0.18)
    return jnp.clip(array, -most, most).astype(held_as)


def setup_inputs(seed: int = 0, part: int = 0) -> dict:
    keys = jax.random.split(jax.random.key(seed), 8)
    part_keys = jax.random.split(jax.random.fold_in(keys[7], part), 8)
    return {
        "slab": centred(part_keys[0], (P_SIZE, NR, NC), 1.0, 6.0, ((0, 2), (1, 4), (2, 2)), jnp.float32),
        "plane_test": centred(keys[1], (P_SIZE, K), P_SIZE ** -0.5, 4.0, ((0, 2),), jnp.float32),
        "row_test": centred(keys[2], (NR, K), NR ** -0.5, 0.25, ((0, 4),), jnp.float32),
        "col_test": centred(keys[3], (NC, K), NC ** -0.5, 0.1875, ((0, 2),), jnp.float32),
        "core_planes": centred(keys[4], (S, P_SIZE), P_SIZE ** -0.5, 4.0, ((0, 2),), jnp.float32),
        "core_rows": centred(keys[5], (S, NR), NR ** -0.5, 0.25, ((1, 4),), jnp.float32),
        "core_cols": centred(keys[6], (S, NC), NC ** -0.5, 0.1875, ((1, 2),), jnp.float32),
    }


def reference(slab, plane_test, row_test, col_test, core_planes, core_rows, core_cols):
    highest = lax.Precision.HIGHEST
    by_col = jnp.einsum('pij,jr->pir', slab, col_test, precision=highest)
    plane_sketch = jnp.einsum('pir,ir->pr', by_col, row_test, precision=highest)
    row_sketch = jnp.einsum('pir,pr->ir', by_col, plane_test, precision=highest)
    by_row = jnp.einsum('pij,ir->pjr', slab, row_test, precision=highest)
    col_sketch = jnp.einsum('pjr,pr->jr', by_row, plane_test, precision=highest)
    shrunk = jnp.einsum('pij,bj->pib', slab, core_cols, precision=highest)
    partial_value = jnp.einsum('pib,ai->pab', shrunk, core_rows, precision=highest)
    core_sketch = jnp.einsum('cp,pab->cab', core_planes, partial_value, precision=highest)
    return plane_sketch, row_sketch, col_sketch, core_sketch
```

```python
import functools

import jax
import jax.numpy as jnp
from jax import lax
from jax.experimental import pallas as pl
from jax.experimental.pallas import tpu as pltpu
from jax.sharding import PartitionSpec as P

F32 = jnp.float32
MESH = pl.DeviceIdType.MESH


def split(x):
    high = x.astype(jnp.bfloat16)
    return high, (x - high.astype(F32)).astype(jnp.bfloat16)


def dot3(a, b, dims):
    f = functools.partial(
        lax.dot_general, dimension_numbers=(dims, ((), ())), preferred_element_type=F32
    )
    return f(a[0], b[0]) + (f(a[0], b[1]) + f(a[1], b[0]))


NN = ((1,), (0,))
NT = ((1,), (1,))


def exchange_kernel(
    nx, ny, nz,
    slab_ref, plane_test_ref, row_test_ref, col_test_ref, core_rows_ref, core_cols_ref,
    gathered_ref, row_ref, col_ref, plane_ref,
    shrunk, shrunk_in, part, part_in, full, full_in,
    row_a, row_a_in, row_b, row_b_in,
    col_a, col_a_in, col_b, col_b_in,
    plane_a, plane_a_in, plane_b, plane_b_in,
    send_sem, recv_sem,
):
    size = {"bx": nx, "by": ny, "bz": nz}
    me = {name: lax.axis_index(name) for name in size}
    count = [0]

    def peer(name, d):
        return lax.rem(me[name] + d, size[name])

    barrier = pltpu.get_barrier_semaphore()
    for name in size:
        for d in range(1, size[name]):
            pl.semaphore_signal(barrier, inc=1, device_id={name: peer(name, d)}, device_id_type=MESH)

    def send(name, d, src, dst):
        n = count[0]
        count[0] += 1
        copy = pltpu.make_async_remote_copy(
            src_ref=src, dst_ref=dst, send_sem=send_sem.at[n], recv_sem=recv_sem.at[n],
            device_id={name: peer(name, d)}, device_id_type=MESH,
        )
        copy.start()
        return copy

    copies = []

    def send_all(name, source, landing):
        group = [send(name, d, source(d), landing.at[d - 1]) for d in range(1, size[name])]
        copies.extend(group)
        return group

    def arrived(group):
        for copy in group:
            copy.wait_recv()

    slab = split(slab_ref[0])
    wide = shrunk.shape[2]
    for y in range(ny):
        shrunk[y] = dot3(slab, split(core_cols_ref[y * wide:(y + 1) * wide, :]), NT)
    pl.semaphore_wait(barrier, nx + ny + nz - 3)
    shrunk_sent = send_all("by", lambda d: shrunk.at[peer("by", d)], shrunk_in)

    row_test = row_test_ref[...]
    plane_test = plane_test_ref[...]
    scaled = split((row_test * plane_test).T)
    terms = dot3(scaled, slab, NN)
    block = col_a.shape[2]
    for x in range(nx):
        for z in range(nz):
            first = (x * nz + z) * block
            col_a[z, x] = terms[first:first + block, :]
    col_a_sent = send_all("bz", lambda d: col_a.at[peer("bz", d)], col_a_in)

    by_col = dot3(slab, split(col_test_ref[...]), NN)
    plane_a[...] = jnp.sum(by_col * row_test, axis=0, keepdims=True)
    plane_a_sent = send_all("by", lambda d: plane_a, plane_a_in)
    terms = (by_col * plane_test).T
    block = row_a.shape[2]
    for y in range(ny):
        for z in range(nz):
            first = (y * nz + z) * block
            row_a[z, y] = terms[first:first + block, :]
    row_a_sent = send_all("bz", lambda d: row_a.at[peer("bz", d)], row_a_in)

    arrived(col_a_sent)
    total = col_a[me["bz"]]
    for d in range(1, nz):
        total = total + col_a_in[d - 1]
    col_b[...] = total
    col_b_sent = send_all("bx", lambda d: col_b.at[peer("bx", d)], col_b_in)

    arrived(shrunk_sent)
    total = shrunk[me["by"]]
    for d in range(1, ny):
        total = total + shrunk_in[d - 1]
    reduced = split(total)
    tall = part.shape[1]
    part_sent = []
    for d in range(1, nx + 1):
        to = peer("bx", d)
        rows = core_rows_ref[pl.ds(pl.multiple_of(to * tall, tall), tall), :]
        part[d - 1] = dot3(split(rows), reduced, NN)
        if d < nx:
            part_sent.append(send("bx", d, part.at[d - 1], part_in.at[d - 1]))
    copies.extend(part_sent)

    arrived(row_a_sent)
    total = row_a[me["bz"]]
    for d in range(1, nz):
        total = total + row_a_in[d - 1]
    row_b[...] = total
    row_b_sent = send_all("by", lambda d: row_b.at[peer("by", d)], row_b_in)

    arrived(plane_a_sent)
    total = plane_a[...]
    for d in range(1, ny):
        total = total + plane_a_in[d - 1]
    plane_b[...] = total
    plane_b_sent = send_all("bx", lambda d: plane_b, plane_b_in)

    arrived(row_b_sent)
    total = row_b[me["by"]]
    for d in range(1, ny):
        total = total + row_b_in[d - 1]
    row_ref[...] = total

    arrived(col_b_sent)
    total = col_b[me["bx"]]
    for d in range(1, nx):
        total = total + col_b_in[d - 1]
    col_ref[...] = total

    total = part[nx - 1]
    for d in range(1, nx):
        part_sent[d - 1].wait_recv()
        total = total + part_in[d - 1]
    full[...] = total
    full_sent = send_all("bz", lambda d: full, full_in)
    gathered_ref[me["bz"]] = total

    arrived(plane_b_sent)
    total = plane_b[...]
    for d in range(1, nx):
        total = total + plane_b_in[d - 1]
    plane_ref[...] = total

    arrived(full_sent)
    for d in range(1, nz):
        gathered_ref[lax.rem(me["bz"] + (nz - d), nz)] = full_in[d - 1]
    for copy in copies:
        copy.wait_send()


def core_kernel(planes_ref, gathered_ref, out_ref):
    step = pl.program_id(0)
    rows = out_ref.shape[0]
    for c in range(rows):
        row = step * rows + c
        value = planes_ref[row, 0] * gathered_ref[0]
        for p in range(1, gathered_ref.shape[0]):
            value = value + planes_ref[row, p] * gathered_ref[p]
        out_ref[c] = value


def on_device(nx, ny, nz, slab, plane_test, row_test, col_test, core_planes, core_rows, core_cols):
    rank = row_test.shape[1]
    ni, nj = slab.shape[1:]
    ab, bb = core_rows.shape[0] // nx, core_cols.shape[0] // ny
    rb, cb = rank // (ny * nz), rank // (nx * nz)
    shape = lambda *dims: jax.ShapeDtypeStruct(dims, F32)
    vmem = lambda *dims: pltpu.VMEM(dims, F32)
    transfers = 3 * (nz - 1) + 3 * (ny - 1) + 3 * (nx - 1)
    gathered, row_t, col_t, plane_sketch = pl.pallas_call(
        functools.partial(exchange_kernel, nx, ny, nz),
        out_shape=(shape(nz, ab, bb), shape(rb, ni), shape(cb, nj), shape(1, rank)),
        in_specs=[pl.BlockSpec(memory_space=pltpu.VMEM)] * 6,
        out_specs=[pl.BlockSpec(memory_space=pltpu.VMEM)] * 4,
        scratch_shapes=[
            vmem(ny, ni, bb), vmem(ny - 1, ni, bb),
            vmem(nx, ab, bb), vmem(nx - 1, ab, bb),
            vmem(ab, bb), vmem(nz - 1, ab, bb),
            vmem(nz, ny, rb, ni), vmem(nz - 1, ny, rb, ni),
            vmem(ny, rb, ni), vmem(ny - 1, rb, ni),
            vmem(nz, nx, cb, nj), vmem(nz - 1, nx, cb, nj),
            vmem(nx, cb, nj), vmem(nx - 1, cb, nj),
            vmem(1, rank), vmem(ny - 1, 1, rank),
            vmem(1, rank), vmem(nx - 1, 1, rank),
            pltpu.SemaphoreType.DMA((transfers,)),
            pltpu.SemaphoreType.DMA((transfers,)),
        ],
        compiler_params=pltpu.CompilerParams(
            collective_id=0, has_side_effects=True, vmem_limit_bytes=32 << 20
        ),
        name="exchange",
    )(slab, plane_test, row_test, col_test, core_rows, core_cols)
    depth = core_planes.shape[0]
    rows = min(depth, max(1, (1 << 19) // (ab * bb)))
    core_sketch = pl.pallas_call(
        core_kernel,
        grid=(depth // rows,),
        out_shape=shape(depth, ab, bb),
        in_specs=[
            pl.BlockSpec(memory_space=pltpu.SMEM),
            pl.BlockSpec((nz, ab, bb), lambda i: (0, 0, 0)),
        ],
        out_specs=pl.BlockSpec((rows, ab, bb), lambda i: (i, 0, 0)),
        compiler_params=pltpu.CompilerParams(vmem_limit_bytes=32 << 20),
        name="core",
    )(core_planes, gathered)
    return plane_sketch, row_t.T, col_t.T, core_sketch


def solution(mesh):
    in_specs = (
        P(("groups", "bz"), "bx", "by"),
        P("bz", None),
        P("bx", None),
        P("by", None),
        P("bz", None),
        P(None, "bx"),
        P(None, "by"),
    )
    out_specs = (
        P(("groups", "bz"), None),
        P(("groups", "bx"), ("by", "bz")),
        P(("groups", "by"), ("bx", "bz")),
        P(("groups", "bz"), "bx", "by"),
    )
    sizes = [mesh.shape[name] for name in ("bx", "by", "bz")]
    return jax.shard_map(
        functools.partial(on_device, *sizes),
        mesh=mesh, in_specs=in_specs, out_specs=out_specs, check_vma=False,
    )
```

```python
import functools

import jax
import jax.numpy as jnp
from jax import lax
from jax.experimental import pallas as pl
from jax.experimental.pallas import tpu as pltpu
from jax.sharding import PartitionSpec as P

F32 = jnp.float32
MESH = pl.DeviceIdType.MESH


def split(x):
    high = x.astype(jnp.bfloat16)
    return high, (x - high.astype(F32)).astype(jnp.bfloat16)


def dot3(a, b, dims):
    f = functools.partial(
        lax.dot_general, dimension_numbers=(dims, ((), ())), preferred_element_type=F32
    )
    return f(a[0], b[0]) + (f(a[0], b[1]) + f(a[1], b[0]))


NN = ((1,), (0,))
NT = ((1,), (1,))


def exchange_kernel(
    nx, ny, nz,
    slab_hbm, plane_test_hbm, row_test_hbm, col_test_hbm, core_rows_hbm, core_cols_hbm,
    gathered_ref, row_ref, col_ref, plane_ref,
    slab_ref, plane_test_ref, row_test_ref, col_test_ref, core_rows_ref, core_cols_ref,
    shrunk, shrunk_in, part, part_in, full, full_in,
    row_a, row_a_in, row_b, row_b_in,
    col_a, col_a_in, col_b, col_b_in,
    plane_a, plane_a_in, plane_b, plane_b_in,
    send_sem, recv_sem, load_sem,
):
    size = {"bx": nx, "by": ny, "bz": nz}
    me = {name: lax.axis_index(name) for name in size}
    count = [0]

    loads = {}
    order = (
        (core_cols_hbm, core_cols_ref), (slab_hbm, slab_ref), (row_test_hbm, row_test_ref),
        (plane_test_hbm, plane_test_ref), (core_rows_hbm, core_rows_ref), (col_test_hbm, col_test_ref),
    )
    for n, (source, target) in enumerate(order):
        loads[n] = pltpu.make_async_copy(source, target, load_sem.at[n])
        loads[n].start()

    def peer(name, d):
        return lax.rem(me[name] + d, size[name])

    barrier = pltpu.get_barrier_semaphore()
    for name in size:
        for d in range(1, size[name]):
            pl.semaphore_signal(barrier, inc=1, device_id={name: peer(name, d)}, device_id_type=MESH)

    copies = []

    def send(name, d, src, dst):
        n = count[0]
        count[0] += 1
        copy = pltpu.make_async_remote_copy(
            src_ref=src, dst_ref=dst, send_sem=send_sem.at[n], recv_sem=recv_sem.at[n],
            device_id={name: peer(name, d)}, device_id_type=MESH,
        )
        copy.start()
        copies.append(copy)
        return copy

    def send_all(name, source, landing):
        return [send(name, d, source(d), landing(d - 1)) for d in range(1, size[name])]

    def arrived(group):
        for copy in group:
            copy.wait_recv()

    loads[0].wait()
    loads[1].wait()
    slab = split(slab_ref[0])
    chunks, ni, wide = shrunk.shape[1:]

    def shrink(h):
        rows = [
            core_cols_ref[(y * chunks + h) * wide:(y * chunks + h + 1) * wide, :] for y in range(ny)
        ]
        terms = dot3(slab, split(jnp.concatenate(rows, axis=0)), NT)
        for y in range(ny):
            shrunk[y, h] = terms[:, y * wide:(y + 1) * wide]

    def send_shrunk(h):
        return send_all("by", lambda d: shrunk.at[peer("by", d), h], lambda n: shrunk_in.at[n, h])

    shrunk_sent = []
    shrink(0)
    pl.semaphore_wait(barrier, nx + ny + nz - 3)
    shrunk_sent.append(send_shrunk(0))

    loads[2].wait()
    loads[3].wait()
    row_test = row_test_ref[...]
    plane_test = plane_test_ref[...]
    scaled = split((row_test * plane_test).T)
    terms = dot3(scaled, slab, NN)
    block = col_a.shape[2]
    for x in range(nx):
        for z in range(nz):
            first = (x * nz + z) * block
            col_a[z, x] = terms[first:first + block, :]
    col_a_sent = send_all("bz", lambda d: col_a.at[peer("bz", d)], lambda n: col_a_in.at[n])

    for h in range(1, chunks):
        shrink(h)
        shrunk_sent.append(send_shrunk(h))

    loads[4].wait()
    tall = part.shape[2]
    part_sent = []

    def send_part(h):
        arrived(shrunk_sent[h])
        total = shrunk[me["by"], h]
        for d in range(1, ny):
            total = total + shrunk_in[d - 1, h]
        reduced = split(total)
        group = []
        for d in range(1, nx + 1):
            to = peer("bx", d)
            rows = core_rows_ref[pl.ds(pl.multiple_of(to * tall, tall), tall), :]
            part[d - 1, h] = dot3(split(rows), reduced, NN)
            if d < nx:
                group.append(send("bx", d, part.at[d - 1, h], part_in.at[d - 1, h]))
        part_sent.append(group)

    send_part(0)

    arrived(col_a_sent)
    total = col_a[me["bz"]]
    for d in range(1, nz):
        total = total + col_a_in[d - 1]
    col_b[...] = total
    col_b_sent = send_all("bx", lambda d: col_b.at[peer("bx", d)], lambda n: col_b_in.at[n])

    for h in range(1, chunks):
        send_part(h)

    loads[5].wait()
    by_col = dot3(slab, split(col_test_ref[...]), NN)
    plane_a[...] = jnp.sum(by_col * row_test, axis=0, keepdims=True)
    plane_a_sent = send_all("by", lambda d: plane_a, lambda n: plane_a_in.at[n])
    terms = (by_col * plane_test).T
    block = row_a.shape[2]
    for y in range(ny):
        for z in range(nz):
            first = (y * nz + z) * block
            row_a[z, y] = terms[first:first + block, :]
    row_a_sent = send_all("bz", lambda d: row_a.at[peer("bz", d)], lambda n: row_a_in.at[n])

    arrived(plane_a_sent)
    total = plane_a[...]
    for d in range(1, ny):
        total = total + plane_a_in[d - 1]
    plane_b[...] = total
    plane_b_sent = send_all("bx", lambda d: plane_b, lambda n: plane_b_in.at[n])

    arrived(row_a_sent)
    total = row_a[me["bz"]]
    for d in range(1, nz):
        total = total + row_a_in[d - 1]
    row_b[...] = total
    row_b_sent = send_all("by", lambda d: row_b.at[peer("by", d)], lambda n: row_b_in.at[n])

    def finish_part(h):
        total = part[nx - 1, h]
        for d in range(1, nx):
            part_sent[h][d - 1].wait_recv()
            total = total + part_in[d - 1, h]
        full[h] = total
        gathered_ref[me["bz"], :, h * wide:(h + 1) * wide] = total
        return send_all("bz", lambda d: full.at[h], lambda n: full_in.at[n, h])

    full_sent = [finish_part(0)]

    arrived(row_b_sent)
    total = row_b[me["by"]]
    for d in range(1, ny):
        total = total + row_b_in[d - 1]
    row_ref[...] = total

    arrived(col_b_sent)
    total = col_b[me["bx"]]
    for d in range(1, nx):
        total = total + col_b_in[d - 1]
    col_ref[...] = total

    for h in range(1, chunks):
        full_sent.append(finish_part(h))

    arrived(plane_b_sent)
    total = plane_b[...]
    for d in range(1, nx):
        total = total + plane_b_in[d - 1]
    plane_ref[...] = total

    for h in range(chunks):
        arrived(full_sent[h])
        for d in range(1, nz):
            gathered_ref[peer("bz", nz - d), :, h * wide:(h + 1) * wide] = full_in[d - 1, h]
    for copy in copies:
        copy.wait_send()


def core_kernel(
    planes_ref, gathered_ref, row_in, col_in, plane_in,
    row_ref, col_ref, plane_ref, out_ref,
    slots, out_sem, small_sem,
):
    count, rows = slots.shape[:2]
    steps = out_ref.shape[0] // rows
    small = [
        pltpu.make_async_copy(source, target, small_sem.at[n])
        for n, (source, target) in enumerate(
            ((row_in, row_ref), (col_in, col_ref), (plane_in, plane_ref))
        )
    ]

    def copy(step, slot):
        return pltpu.make_async_copy(
            slots.at[slot], out_ref.at[pl.ds(step * rows, rows)], out_sem.at[slot]
        )

    def body(step, _):
        slot = lax.rem(step, count)

        @pl.when(step >= count)
        def _():
            copy(step - count, slot).wait()

        for c in range(rows):
            row = step * rows + c
            value = planes_ref[0, row] * gathered_ref[0]
            for p in range(1, gathered_ref.shape[0]):
                value = value + planes_ref[p, row] * gathered_ref[p]
            slots[slot, c] = value
        copy(step, slot).start()
        return 0

    lax.fori_loop(0, steps, body, 0)
    for one in small:
        one.start()
    for step in range(steps - count, steps):
        copy(step, step % count).wait()
    for one in small:
        one.wait()


def on_device(nx, ny, nz, slab, plane_test, row_test, col_test, core_planes, core_rows, core_cols):
    rank = row_test.shape[1]
    ni, nj = slab.shape[1:]
    ab, bb = core_rows.shape[0] // nx, core_cols.shape[0] // ny
    rb, cb = rank // (ny * nz), rank // (nx * nz)
    chunks = 2 if bb % 256 == 0 else 1
    wide = bb // chunks
    shape = lambda *dims: jax.ShapeDtypeStruct(dims, F32)
    vmem = lambda *dims: pltpu.VMEM(dims, F32)
    inputs = (slab, plane_test, row_test, col_test, core_rows, core_cols)
    transfers = (2 + chunks) * (nz - 1) + (2 + chunks) * (ny - 1) + (2 + chunks) * (nx - 1)
    gathered, row_t, col_t, plane_sketch = pl.pallas_call(
        functools.partial(exchange_kernel, nx, ny, nz),
        out_shape=(shape(nz, ab, bb), shape(rb, ni), shape(cb, nj), shape(1, rank)),
        in_specs=[pl.BlockSpec(memory_space=pltpu.HBM)] * 6,
        out_specs=[pl.BlockSpec(memory_space=pltpu.VMEM)] * 4,
        scratch_shapes=[vmem(*a.shape) for a in inputs] + [
            vmem(ny, chunks, ni, wide), vmem(ny - 1, chunks, ni, wide),
            vmem(nx, chunks, ab, wide), vmem(nx - 1, chunks, ab, wide),
            vmem(chunks, ab, wide), vmem(nz - 1, chunks, ab, wide),
            vmem(nz, ny, rb, ni), vmem(nz - 1, ny, rb, ni),
            vmem(ny, rb, ni), vmem(ny - 1, rb, ni),
            vmem(nz, nx, cb, nj), vmem(nz - 1, nx, cb, nj),
            vmem(nx, cb, nj), vmem(nx - 1, cb, nj),
            vmem(1, rank), vmem(ny - 1, 1, rank),
            vmem(1, rank), vmem(nx - 1, 1, rank),
            pltpu.SemaphoreType.DMA((transfers,)),
            pltpu.SemaphoreType.DMA((transfers,)),
            pltpu.SemaphoreType.DMA((len(inputs),)),
        ],
        compiler_params=pltpu.CompilerParams(
            collective_id=0, has_side_effects=True, vmem_limit_bytes=32 << 20
        ),
        name="exchange",
    )(*(pltpu.with_memory_space_constraint(a, pltpu.HBM) for a in inputs))
    depth = core_planes.shape[0]
    rows = min(depth, max(1, (1 << 17) // (ab * bb)))
    slots = min(8, depth // rows)
    row_t, col_t, plane_sketch, core_sketch = pl.pallas_call(
        core_kernel,
        out_shape=(shape(rb, ni), shape(cb, nj), shape(1, rank), shape(depth, ab, bb)),
        in_specs=[pl.BlockSpec(memory_space=pltpu.SMEM)]
        + [pl.BlockSpec(memory_space=pltpu.VMEM)] * 4,
        out_specs=[pl.BlockSpec(memory_space=pltpu.HBM)] * 4,
        scratch_shapes=[
            vmem(slots, rows, ab, bb),
            pltpu.SemaphoreType.DMA((slots,)),
            pltpu.SemaphoreType.DMA((3,)),
        ],
        compiler_params=pltpu.CompilerParams(vmem_limit_bytes=16 << 20),
        name="core",
    )(core_planes.T, gathered, row_t, col_t, plane_sketch)
    return plane_sketch, row_t.T, col_t.T, core_sketch


def solution(mesh):
    in_specs = (
        P(("groups", "bz"), "bx", "by"),
        P("bz", None),
        P("bx", None),
        P("by", None),
        P("bz", None),
        P(None, "bx"),
        P(None, "by"),
    )
    out_specs = (
        P(("groups", "bz"), None),
        P(("groups", "bx"), ("by", "bz")),
        P(("groups", "by"), ("bx", "bz")),
        P(("groups", "bz"), "bx", "by"),
    )
    sizes = [mesh.shape[name] for name in ("bx", "by", "bz")]
    return jax.shard_map(
        functools.partial(on_device, *sizes),
        mesh=mesh, in_specs=in_specs, out_specs=out_specs, check_vma=False,
    )
```

```python
import functools

import jax
import jax.numpy as jnp
from jax import lax
from jax.experimental import pallas as pl
from jax.experimental.pallas import tpu as pltpu
from jax.sharding import PartitionSpec as P

F32 = jnp.float32
MESH = pl.DeviceIdType.MESH


def split(x):
    high = x.astype(jnp.bfloat16)
    return high, (x - high.astype(F32)).astype(jnp.bfloat16)


def dot3(a, b, dims):
    f = functools.partial(
        lax.dot_general, dimension_numbers=(dims, ((), ())), preferred_element_type=F32
    )
    return f(a[0], b[0]) + (f(a[0], b[1]) + f(a[1], b[0]))


NN = ((1,), (0,))
NT = ((1,), (1,))


def exchange_kernel(
    nx, ny, nz,
    slab_hbm, plane_test_hbm, row_test_hbm, col_test_hbm, core_rows_hbm, core_cols_hbm,
    *refs,
):
    gathered_ref, row_ref, plane_ref = refs[:3]
    col_refs = refs[3:3 + nx]
    exchange_body(
        nx, ny, nz,
        slab_hbm, plane_test_hbm, row_test_hbm, col_test_hbm, core_rows_hbm, core_cols_hbm,
        gathered_ref, row_ref, col_refs, plane_ref, *refs[3 + nx:],
    )


def exchange_body(
    nx, ny, nz,
    slab_hbm, plane_test_hbm, row_test_hbm, col_test_hbm, core_rows_hbm, core_cols_hbm,
    gathered_ref, row_ref, col_refs, plane_ref,
    slab_ref, plane_test_ref, row_test_ref, col_test_ref, core_rows_ref, core_cols_ref,
    shrunk, shrunk_in, part, part_in, full, full_in,
    row_a, row_a_in, row_b, row_b_in,
    col_a, col_a_in,
    plane_a, plane_a_in, plane_b, plane_b_in,
    send_sem, recv_sem, load_sem,
):
    size = {"bx": nx, "by": ny, "bz": nz}
    me = {name: lax.axis_index(name) for name in size}
    count = [0]

    loads = {}
    order = (
        (core_cols_hbm, core_cols_ref), (slab_hbm, slab_ref), (row_test_hbm, row_test_ref),
        (plane_test_hbm, plane_test_ref), (core_rows_hbm, core_rows_ref), (col_test_hbm, col_test_ref),
    )
    for n, (source, target) in enumerate(order):
        loads[n] = pltpu.make_async_copy(source, target, load_sem.at[n])
        loads[n].start()

    def peer(name, d):
        return lax.rem(me[name] + d, size[name])

    barrier = pltpu.get_barrier_semaphore()
    for name in size:
        for d in range(1, size[name]):
            pl.semaphore_signal(barrier, inc=1, device_id={name: peer(name, d)}, device_id_type=MESH)

    copies = []

    def send(name, d, src, dst):
        n = count[0]
        count[0] += 1
        copy = pltpu.make_async_remote_copy(
            src_ref=src, dst_ref=dst, send_sem=send_sem.at[n], recv_sem=recv_sem.at[n],
            device_id={name: peer(name, d)}, device_id_type=MESH,
        )
        copy.start()
        copies.append(copy)
        return copy

    def send_all(name, source, landing):
        return [send(name, d, source(d), landing(d - 1)) for d in range(1, size[name])]

    def arrived(group):
        for copy in group:
            copy.wait_recv()

    loads[0].wait()
    loads[1].wait()
    slab = split(slab_ref[0])
    chunks, ni, wide = shrunk.shape[1:]

    def shrink(h):
        rows = [
            core_cols_ref[(y * chunks + h) * wide:(y * chunks + h + 1) * wide, :] for y in range(ny)
        ]
        terms = dot3(slab, split(jnp.concatenate(rows, axis=0)), NT)
        for y in range(ny):
            shrunk[y, h] = terms[:, y * wide:(y + 1) * wide]

    def send_shrunk(h):
        return send_all("by", lambda d: shrunk.at[peer("by", d), h], lambda n: shrunk_in.at[n, h])

    shrunk_sent = []
    shrink(0)
    pl.semaphore_wait(barrier, nx + ny + nz - 3)
    shrunk_sent.append(send_shrunk(0))

    loads[2].wait()
    loads[3].wait()
    row_test = row_test_ref[...]
    plane_test = plane_test_ref[...]
    scaled = split((row_test * plane_test).T)
    terms = dot3(scaled, slab, NN)
    block = col_a.shape[2]
    for x in range(nx):
        for z in range(nz):
            first = (x * nz + z) * block
            col_a[z, x] = terms[first:first + block, :]
    col_a_sent = send_all("bz", lambda d: col_a.at[peer("bz", d)], lambda n: col_a_in.at[n])

    for h in range(1, chunks):
        shrink(h)
        shrunk_sent.append(send_shrunk(h))

    loads[4].wait()
    tall = part.shape[2]
    part_sent = []

    def send_part(h):
        arrived(shrunk_sent[h])
        total = shrunk[me["by"], h]
        for d in range(1, ny):
            total = total + shrunk_in[d - 1, h]
        reduced = split(total)
        group = []
        for d in range(1, nx + 1):
            to = peer("bx", d)
            rows = core_rows_ref[pl.ds(pl.multiple_of(to * tall, tall), tall), :]
            part[d - 1, h] = dot3(split(rows), reduced, NN)
            if d < nx:
                group.append(send("bx", d, part.at[d - 1, h], part_in.at[d - 1, h]))
        part_sent.append(group)

    send_part(0)

    for h in range(1, chunks):
        send_part(h)

    loads[5].wait()
    by_col = dot3(slab, split(col_test_ref[...]), NN)
    plane_a[...] = jnp.sum(by_col * row_test, axis=0, keepdims=True)
    plane_a_sent = send_all("by", lambda d: plane_a, lambda n: plane_a_in.at[n])
    terms = (by_col * plane_test).T
    block = row_a.shape[2]
    for y in range(ny):
        for z in range(nz):
            first = (y * nz + z) * block
            row_a[z, y] = terms[first:first + block, :]
    row_a_sent = send_all("bz", lambda d: row_a.at[peer("bz", d)], lambda n: row_a_in.at[n])

    arrived(plane_a_sent)
    total = plane_a[...]
    for d in range(1, ny):
        total = total + plane_a_in[d - 1]
    plane_b[...] = total
    plane_b_sent = send_all("bx", lambda d: plane_b, lambda n: plane_b_in.at[n])

    arrived(row_a_sent)
    total = row_a[me["bz"]]
    for d in range(1, nz):
        total = total + row_a_in[d - 1]
    row_b[...] = total
    row_b_sent = send_all("by", lambda d: row_b.at[peer("by", d)], lambda n: row_b_in.at[n])

    def finish_part(h):
        total = part[nx - 1, h]
        for d in range(1, nx):
            part_sent[h][d - 1].wait_recv()
            total = total + part_in[d - 1, h]
        full[h] = total
        gathered_ref[me["bz"], :, h * wide:(h + 1) * wide] = total
        return send_all("bz", lambda d: full.at[h], lambda n: full_in.at[n, h])

    full_sent = [finish_part(0)]

    arrived(row_b_sent)
    total = row_b[me["by"]]
    for d in range(1, ny):
        total = total + row_b_in[d - 1]
    row_ref[...] = total

    arrived(col_a_sent)
    for d in range(nx):
        total = col_a[me["bz"], peer("bx", d)]
        for n in range(nz - 1):
            total = total + col_a_in[n, peer("bx", d)]
        col_refs[d][...] = total

    for h in range(1, chunks):
        full_sent.append(finish_part(h))

    arrived(plane_b_sent)
    total = plane_b[...]
    for d in range(1, nx):
        total = total + plane_b_in[d - 1]
    plane_ref[...] = total

    for h in range(chunks):
        arrived(full_sent[h])
        for d in range(1, nz):
            gathered_ref[peer("bz", nz - d), :, h * wide:(h + 1) * wide] = full_in[d - 1, h]
    for copy in copies:
        copy.wait_send()


def core_kernel(
    planes_ref, gathered_ref, row_in, plane_in,
    row_ref, plane_ref, out_ref,
    slots, out_sem, small_sem,
):
    count, rows = slots.shape[:2]
    steps = out_ref.shape[0] // rows
    small = [
        pltpu.make_async_copy(source, target, small_sem.at[n])
        for n, (source, target) in enumerate(
            ((row_in, row_ref), (plane_in, plane_ref))
        )
    ]

    def copy(step, slot):
        return pltpu.make_async_copy(
            slots.at[slot], out_ref.at[pl.ds(step * rows, rows)], out_sem.at[slot]
        )

    def body(step, _):
        slot = lax.rem(step, count)

        @pl.when(step >= count)
        def _():
            copy(step - count, slot).wait()

        for c in range(rows):
            row = step * rows + c
            value = planes_ref[0, row] * gathered_ref[0]
            for p in range(1, gathered_ref.shape[0]):
                value = value + planes_ref[p, row] * gathered_ref[p]
            slots[slot, c] = value
        copy(step, slot).start()
        return 0

    lax.fori_loop(0, steps, body, 0)
    for one in small:
        one.start()
    for step in range(steps - count, steps):
        copy(step, step % count).wait()
    for one in small:
        one.wait()


def on_device(nx, ny, nz, slab, plane_test, row_test, col_test, core_planes, core_rows, core_cols):
    rank = row_test.shape[1]
    ni, nj = slab.shape[1:]
    ab, bb = core_rows.shape[0] // nx, core_cols.shape[0] // ny
    rb, cb = rank // (ny * nz), rank // (nx * nz)
    chunks = 2 if bb % 256 == 0 else 1
    wide = bb // chunks
    shape = lambda *dims: jax.ShapeDtypeStruct(dims, F32)
    vmem = lambda *dims: pltpu.VMEM(dims, F32)
    inputs = (slab, plane_test, row_test, col_test, core_rows, core_cols)
    transfers = (2 + chunks) * (nz - 1) + (2 + chunks) * (ny - 1) + (1 + chunks) * (nx - 1)
    gathered, row_t, plane_sketch, *col_terms = pl.pallas_call(
        functools.partial(exchange_kernel, nx, ny, nz),
        out_shape=(shape(nz, ab, bb), shape(rb, ni), shape(1, rank)) + (shape(cb, nj),) * nx,
        in_specs=[pl.BlockSpec(memory_space=pltpu.HBM)] * 6,
        out_specs=[pl.BlockSpec(memory_space=pltpu.VMEM)] * (3 + nx),
        scratch_shapes=[vmem(*a.shape) for a in inputs] + [
            vmem(ny, chunks, ni, wide), vmem(ny - 1, chunks, ni, wide),
            vmem(nx, chunks, ab, wide), vmem(nx - 1, chunks, ab, wide),
            vmem(chunks, ab, wide), vmem(nz - 1, chunks, ab, wide),
            vmem(nz, ny, rb, ni), vmem(nz - 1, ny, rb, ni),
            vmem(ny, rb, ni), vmem(ny - 1, rb, ni),
            vmem(nz, nx, cb, nj), vmem(nz - 1, nx, cb, nj),
            vmem(1, rank), vmem(ny - 1, 1, rank),
            vmem(1, rank), vmem(nx - 1, 1, rank),
            pltpu.SemaphoreType.DMA((transfers,)),
            pltpu.SemaphoreType.DMA((transfers,)),
            pltpu.SemaphoreType.DMA((len(inputs),)),
        ],
        compiler_params=pltpu.CompilerParams(
            collective_id=0, has_side_effects=True, vmem_limit_bytes=32 << 20
        ),
        name="exchange",
    )(*(pltpu.with_memory_space_constraint(a, pltpu.HBM) for a in inputs))
    depth = core_planes.shape[0]
    rows = min(depth, max(1, (1 << 17) // (ab * bb)))
    slots = min(8, depth // rows)
    col_t = col_terms[0]
    for d in range(1, nx):
        col_t = col_t + lax.ppermute(col_terms[d], "bx", [(x, (x + d) % nx) for x in range(nx)])
    row_t, plane_sketch, core_sketch = pl.pallas_call(
        core_kernel,
        out_shape=(shape(rb, ni), shape(1, rank), shape(depth, ab, bb)),
        in_specs=[pl.BlockSpec(memory_space=pltpu.SMEM)]
        + [pl.BlockSpec(memory_space=pltpu.VMEM)] * 3,
        out_specs=[pl.BlockSpec(memory_space=pltpu.HBM)] * 3,
        scratch_shapes=[
            vmem(slots, rows, ab, bb),
            pltpu.SemaphoreType.DMA((slots,)),
            pltpu.SemaphoreType.DMA((2,)),
        ],
        compiler_params=pltpu.CompilerParams(vmem_limit_bytes=16 << 20),
        cost_estimate=pl.CostEstimate(
            flops=4 * depth * ab * bb, bytes_accessed=4 * depth * ab * bb, transcendentals=0
        ),
        name="core",
    )(core_planes.T, gathered, row_t, plane_sketch)
    return plane_sketch, row_t.T, col_t.T, core_sketch


def solution(mesh):
    in_specs = (
        P(("groups", "bz"), "bx", "by"),
        P("bz", None),
        P("bx", None),
        P("by", None),
        P("bz", None),
        P(None, "bx"),
        P(None, "by"),
    )
    out_specs = (
        P(("groups", "bz"), None),
        P(("groups", "bx"), ("by", "bz")),
        P(("groups", "by"), ("bx", "bz")),
        P(("groups", "bz"), "bx", "by"),
    )
    sizes = [mesh.shape[name] for name in ("bx", "by", "bz")]
    return jax.shard_map(
        functools.partial(on_device, *sizes),
        mesh=mesh, in_specs=in_specs, out_specs=out_specs, check_vma=False,
    )
```

```python
import functools

import jax
import jax.numpy as jnp
from jax import lax
from jax.experimental import pallas as pl
from jax.experimental.pallas import tpu as pltpu
from jax.sharding import PartitionSpec as P

F32 = jnp.float32
MESH = pl.DeviceIdType.MESH


def split(x):
    high = x.astype(jnp.bfloat16)
    return high, (x - high.astype(F32)).astype(jnp.bfloat16)


def dot3(a, b, dims):
    f = functools.partial(
        lax.dot_general, dimension_numbers=(dims, ((), ())), preferred_element_type=F32
    )
    return f(a[0], b[0]) + (f(a[0], b[1]) + f(a[1], b[0]))


NN = ((1,), (0,))
NT = ((1,), (1,))


def exchange_kernel(
    nx, ny, nz,
    slab_hbm, plane_test_hbm, row_test_hbm, col_test_hbm, core_rows_hbm, core_cols_hbm,
    *refs,
):
    gathered_ref, row_ref, plane_ref = refs[:3]
    col_ref = refs[3]
    exchange_body(
        nx, ny, nz,
        slab_hbm, plane_test_hbm, row_test_hbm, col_test_hbm, core_rows_hbm, core_cols_hbm,
        gathered_ref, row_ref, col_ref, plane_ref, *refs[4:],
    )


def exchange_body(
    nx, ny, nz,
    slab_hbm, plane_test_hbm, row_test_hbm, col_test_hbm, core_rows_hbm, core_cols_hbm,
    gathered_ref, row_ref, col_ref, plane_ref,
    slab_ref, plane_test_ref, row_test_ref, col_test_ref, core_rows_ref, core_cols_ref,
    shrunk, shrunk_in, part, part_in, full, full_in,
    row_a, row_a_in, row_b, row_b_in,
    col_a, col_a_in,
    plane_a, plane_a_in, plane_b, plane_b_in,
    send_sem, recv_sem, load_sem,
):
    size = {"bx": nx, "by": ny, "bz": nz}
    me = {name: lax.axis_index(name) for name in size}
    count = [0]

    loads = {}
    order = (
        (core_cols_hbm, core_cols_ref), (slab_hbm, slab_ref), (row_test_hbm, row_test_ref),
        (plane_test_hbm, plane_test_ref), (core_rows_hbm, core_rows_ref), (col_test_hbm, col_test_ref),
    )
    for n, (source, target) in enumerate(order):
        loads[n] = pltpu.make_async_copy(source, target, load_sem.at[n])
        loads[n].start()

    def peer(name, d):
        return lax.rem(me[name] + d, size[name])

    barrier = pltpu.get_barrier_semaphore()
    for name in size:
        for d in range(1, size[name]):
            pl.semaphore_signal(barrier, inc=1, device_id={name: peer(name, d)}, device_id_type=MESH)

    copies = []

    def send(name, d, src, dst):
        n = count[0]
        count[0] += 1
        copy = pltpu.make_async_remote_copy(
            src_ref=src, dst_ref=dst, send_sem=send_sem.at[n], recv_sem=recv_sem.at[n],
            device_id={name: peer(name, d)}, device_id_type=MESH,
        )
        copy.start()
        copies.append(copy)
        return copy

    def send_all(name, source, landing):
        return [send(name, d, source(d), landing(d - 1)) for d in range(1, size[name])]

    def arrived(group):
        for copy in group:
            copy.wait_recv()

    loads[0].wait()
    loads[1].wait()
    slab = split(slab_ref[0])
    chunks, ni, wide = shrunk.shape[1:]

    def shrink(h):
        rows = [
            core_cols_ref[(y * chunks + h) * wide:(y * chunks + h + 1) * wide, :] for y in range(ny)
        ]
        terms = dot3(slab, split(jnp.concatenate(rows, axis=0)), NT)
        for y in range(ny):
            shrunk[y, h] = terms[:, y * wide:(y + 1) * wide]

    def send_shrunk(h):
        return send_all("by", lambda d: shrunk.at[peer("by", d), h], lambda n: shrunk_in.at[n, h])

    shrunk_sent = []
    shrink(0)
    pl.semaphore_wait(barrier, nx + ny + nz - 3)
    shrunk_sent.append(send_shrunk(0))

    loads[2].wait()
    loads[3].wait()
    row_test = row_test_ref[...]
    plane_test = plane_test_ref[...]
    scaled = split((row_test * plane_test).T)
    terms = dot3(scaled, slab, NN)
    block = col_a.shape[2]
    for x in range(nx):
        for z in range(nz):
            first = (x * nz + z) * block
            col_a[z, x] = terms[first:first + block, :]
    col_a_sent = send_all("bz", lambda d: col_a.at[peer("bz", d)], lambda n: col_a_in.at[n])

    for h in range(1, chunks):
        shrink(h)
        shrunk_sent.append(send_shrunk(h))

    loads[4].wait()
    tall = part.shape[2]
    part_sent = []

    def send_part(h):
        arrived(shrunk_sent[h])
        total = shrunk[me["by"], h]
        for d in range(1, ny):
            total = total + shrunk_in[d - 1, h]
        reduced = split(total)
        group = []
        for d in range(1, nx + 1):
            to = peer("bx", d)
            rows = core_rows_ref[pl.ds(pl.multiple_of(to * tall, tall), tall), :]
            part[d - 1, h] = dot3(split(rows), reduced, NN)
            if d < nx:
                group.append(send("bx", d, part.at[d - 1, h], part_in.at[d - 1, h]))
        part_sent.append(group)

    send_part(0)

    for h in range(1, chunks):
        send_part(h)

    loads[5].wait()
    by_col = dot3(slab, split(col_test_ref[...]), NN)
    plane_a[...] = jnp.sum(by_col * row_test, axis=0, keepdims=True)
    plane_a_sent = send_all("by", lambda d: plane_a, lambda n: plane_a_in.at[n])
    terms = (by_col * plane_test).T
    block = row_a.shape[2]
    for y in range(ny):
        for z in range(nz):
            first = (y * nz + z) * block
            row_a[z, y] = terms[first:first + block, :]
    row_a_sent = send_all("bz", lambda d: row_a.at[peer("bz", d)], lambda n: row_a_in.at[n])

    arrived(plane_a_sent)
    total = plane_a[...]
    for d in range(1, ny):
        total = total + plane_a_in[d - 1]
    plane_b[...] = total
    plane_b_sent = send_all("bx", lambda d: plane_b, lambda n: plane_b_in.at[n])

    arrived(row_a_sent)
    total = row_a[me["bz"]]
    for d in range(1, nz):
        total = total + row_a_in[d - 1]
    row_b[...] = total
    row_b_sent = send_all("by", lambda d: row_b.at[peer("by", d)], lambda n: row_b_in.at[n])

    def finish_part(h):
        total = part[nx - 1, h]
        for d in range(1, nx):
            part_sent[h][d - 1].wait_recv()
            total = total + part_in[d - 1, h]
        full[h] = total
        gathered_ref[me["bz"], :, h * wide:(h + 1) * wide] = total
        return send_all("bz", lambda d: full.at[h], lambda n: full_in.at[n, h])

    full_sent = [finish_part(0)]

    arrived(row_b_sent)
    total = row_b[me["by"]]
    for d in range(1, ny):
        total = total + row_b_in[d - 1]
    row_ref[...] = total

    arrived(col_a_sent)
    total = col_a[me["bz"]]
    for d in range(1, nz):
        total = total + col_a_in[d - 1]
    col_ref[...] = total

    for h in range(1, chunks):
        full_sent.append(finish_part(h))

    arrived(plane_b_sent)
    total = plane_b[...]
    for d in range(1, nx):
        total = total + plane_b_in[d - 1]
    plane_ref[...] = total

    for h in range(chunks):
        arrived(full_sent[h])
        for d in range(1, nz):
            gathered_ref[peer("bz", nz - d), :, h * wide:(h + 1) * wide] = full_in[d - 1, h]
    for copy in copies:
        copy.wait_send()


def core_kernel(
    planes_ref, gathered_ref, row_in, plane_in,
    row_ref, plane_ref, out_ref,
    slots, out_sem, small_sem,
):
    count, rows = slots.shape[:2]
    steps = out_ref.shape[0] // rows
    small = [
        pltpu.make_async_copy(source, target, small_sem.at[n])
        for n, (source, target) in enumerate(
            ((row_in, row_ref), (plane_in, plane_ref))
        )
    ]

    def copy(step, slot):
        return pltpu.make_async_copy(
            slots.at[slot], out_ref.at[pl.ds(step * rows, rows)], out_sem.at[slot]
        )

    def body(step, _):
        slot = lax.rem(step, count)

        @pl.when(step >= count)
        def _():
            copy(step - count, slot).wait()

        for c in range(rows):
            row = step * rows + c
            value = planes_ref[0, row] * gathered_ref[0]
            for p in range(1, gathered_ref.shape[0]):
                value = value + planes_ref[p, row] * gathered_ref[p]
            slots[slot, c] = value
        copy(step, slot).start()
        return 0

    lax.fori_loop(0, steps, body, 0)
    for one in small:
        one.start()
    for step in range(steps - count, steps):
        copy(step, step % count).wait()
    for one in small:
        one.wait()


def on_device(nx, ny, nz, slab, plane_test, row_test, col_test, core_planes, core_rows, core_cols):
    rank = row_test.shape[1]
    ni, nj = slab.shape[1:]
    ab, bb = core_rows.shape[0] // nx, core_cols.shape[0] // ny
    rb, cb = rank // (ny * nz), rank // (nx * nz)
    chunks = 2 if bb % 256 == 0 else 1
    wide = bb // chunks
    shape = lambda *dims: jax.ShapeDtypeStruct(dims, F32)
    vmem = lambda *dims: pltpu.VMEM(dims, F32)
    inputs = (slab, plane_test, row_test, col_test, core_rows, core_cols)
    transfers = (2 + chunks) * (nz - 1) + (2 + chunks) * (ny - 1) + (1 + chunks) * (nx - 1)
    gathered, row_t, plane_sketch, col_terms = pl.pallas_call(
        functools.partial(exchange_kernel, nx, ny, nz),
        out_shape=(shape(nz, ab, bb), shape(rb, ni), shape(1, rank)) + (shape(nx, cb, nj),),
        in_specs=[pl.BlockSpec(memory_space=pltpu.HBM)] * 6,
        out_specs=[pl.BlockSpec(memory_space=pltpu.VMEM)] * 4,
        scratch_shapes=[vmem(*a.shape) for a in inputs] + [
            vmem(ny, chunks, ni, wide), vmem(ny - 1, chunks, ni, wide),
            vmem(nx, chunks, ab, wide), vmem(nx - 1, chunks, ab, wide),
            vmem(chunks, ab, wide), vmem(nz - 1, chunks, ab, wide),
            vmem(nz, ny, rb, ni), vmem(nz - 1, ny, rb, ni),
            vmem(ny, rb, ni), vmem(ny - 1, rb, ni),
            vmem(nz, nx, cb, nj), vmem(nz - 1, nx, cb, nj),
            vmem(1, rank), vmem(ny - 1, 1, rank),
            vmem(1, rank), vmem(nx - 1, 1, rank),
            pltpu.SemaphoreType.DMA((transfers,)),
            pltpu.SemaphoreType.DMA((transfers,)),
            pltpu.SemaphoreType.DMA((len(inputs),)),
        ],
        compiler_params=pltpu.CompilerParams(
            collective_id=0, has_side_effects=True, vmem_limit_bytes=32 << 20
        ),
        name="exchange",
    )(*(pltpu.with_memory_space_constraint(a, pltpu.HBM) for a in inputs))
    depth = core_planes.shape[0]
    rows = min(depth, max(1, (1 << 17) // (ab * bb)))
    slots = min(8, depth // rows)
    col_t = jnp.sum(lax.all_to_all(col_terms, "bx", 0, 0, tiled=True), axis=0)
    row_t, plane_sketch, core_sketch = pl.pallas_call(
        core_kernel,
        out_shape=(shape(rb, ni), shape(1, rank), shape(depth, ab, bb)),
        in_specs=[pl.BlockSpec(memory_space=pltpu.SMEM)]
        + [pl.BlockSpec(memory_space=pltpu.VMEM)] * 3,
        out_specs=[pl.BlockSpec(memory_space=pltpu.HBM)] * 3,
        scratch_shapes=[
            vmem(slots, rows, ab, bb),
            pltpu.SemaphoreType.DMA((slots,)),
            pltpu.SemaphoreType.DMA((2,)),
        ],
        compiler_params=pltpu.CompilerParams(vmem_limit_bytes=16 << 20),
        cost_estimate=pl.CostEstimate(
            flops=4 * depth * ab * bb, bytes_accessed=4 * depth * ab * bb, transcendentals=0
        ),
        name="core",
    )(core_planes.T, gathered, row_t, plane_sketch)
    return plane_sketch, row_t.T, col_t.T, core_sketch


def solution(mesh):
    in_specs = (
        P(("groups", "bz"), "bx", "by"),
        P("bz", None),
        P("bx", None),
        P("by", None),
        P("bz", None),
        P(None, "bx"),
        P(None, "by"),
    )
    out_specs = (
        P(("groups", "bz"), None),
        P(("groups", "bx"), ("by", "bz")),
        P(("groups", "by"), ("bx", "bz")),
        P(("groups", "bz"), "bx", "by"),
    )
    sizes = [mesh.shape[name] for name in ("bx", "by", "bz")]
    return jax.shard_map(
        functools.partial(on_device, *sizes),
        mesh=mesh, in_specs=in_specs, out_specs=out_specs, check_vma=False,
    )
```

```python
import functools

import jax
import jax.numpy as jnp
from jax import lax
from jax.experimental import pallas as pl
from jax.experimental.pallas import tpu as pltpu
from jax.sharding import PartitionSpec as P

F32 = jnp.float32
MESH = pl.DeviceIdType.MESH


def split(x):
    high = x.astype(jnp.bfloat16)
    return high, (x - high.astype(F32)).astype(jnp.bfloat16)


def dot3(a, b, dims):
    f = functools.partial(
        lax.dot_general, dimension_numbers=(dims, ((), ())), preferred_element_type=F32
    )
    return f(a[0], b[0]) + (f(a[0], b[1]) + f(a[1], b[0]))


NN = ((1,), (0,))
NT = ((1,), (1,))


def exchange_kernel(
    nx, ny, nz,
    slab_hbm, plane_test_hbm, row_test_hbm, col_test_hbm, core_rows_hbm, core_cols_hbm,
    gathered_ref, row_ref, col_ref, plane_ref,
    slab_ref, plane_test_ref, row_test_ref, col_test_ref, core_rows_ref, core_cols_ref,
    shrunk, shrunk_in, part, part_in, full, full_in,
    row_a, row_a_in, row_b, row_b_in,
    col_a, col_a_in, col_b, col_b_in, col_c, col_c_in,
    plane_a, plane_a_in, plane_b, plane_b_in,
    send_sem, recv_sem, load_sem,
):
    size = {"bx": nx, "by": ny, "bz": nz}
    me = {name: lax.axis_index(name) for name in size}
    count = [0]

    loads = {}
    order = (
        (core_cols_hbm, core_cols_ref), (slab_hbm, slab_ref), (row_test_hbm, row_test_ref),
        (plane_test_hbm, plane_test_ref), (core_rows_hbm, core_rows_ref), (col_test_hbm, col_test_ref),
    )
    for n, (source, target) in enumerate(order):
        loads[n] = pltpu.make_async_copy(source, target, load_sem.at[n])
        loads[n].start()

    def peer(name, d):
        return lax.rem(me[name] + d, size[name])

    barrier = pltpu.get_barrier_semaphore()
    for name in size:
        for d in range(1, size[name]):
            pl.semaphore_signal(barrier, inc=1, device_id={name: peer(name, d)}, device_id_type=MESH)

    copies = []

    def send(name, d, src, dst, to=None):
        n = count[0]
        count[0] += 1
        copy = pltpu.make_async_remote_copy(
            src_ref=src, dst_ref=dst, send_sem=send_sem.at[n], recv_sem=recv_sem.at[n],
            device_id={name: peer(name, d) if to is None else to}, device_id_type=MESH,
        )
        copy.start()
        copies.append(copy)
        return copy

    def send_all(name, source, landing):
        return [send(name, d, source(d), landing(d - 1)) for d in range(1, size[name])]

    def arrived(group):
        for copy in group:
            copy.wait_recv()

    loads[0].wait()
    loads[1].wait()
    slab = split(slab_ref[0])
    chunks, ni, wide = shrunk.shape[1:]

    def shrink(h):
        rows = [
            core_cols_ref[(y * chunks + h) * wide:(y * chunks + h + 1) * wide, :] for y in range(ny)
        ]
        terms = dot3(slab, split(jnp.concatenate(rows, axis=0)), NT)
        for y in range(ny):
            shrunk[y, h] = terms[:, y * wide:(y + 1) * wide]

    def send_shrunk(h):
        return send_all("by", lambda d: shrunk.at[peer("by", d), h], lambda n: shrunk_in.at[n, h])

    shrunk_sent = []
    shrink(0)
    pl.semaphore_wait(barrier, nx + ny + nz - 3)
    shrunk_sent.append(send_shrunk(0))

    loads[2].wait()
    loads[3].wait()
    row_test = row_test_ref[...]
    plane_test = plane_test_ref[...]
    scaled = split((row_test * plane_test).T)
    terms = dot3(scaled, slab, NN)
    block = col_a.shape[3]
    for x in range(nx):
        for z in range(nz):
            first = (x * nz + z) * block
            col_a[z, x % 2, x // 2] = terms[first:first + block, :]
    col_a_sent = send_all("bz", lambda d: col_a.at[peer("bz", d)], lambda n: col_a_in.at[n])

    for h in range(1, chunks):
        shrink(h)
        shrunk_sent.append(send_shrunk(h))

    loads[4].wait()
    tall = part.shape[2]
    part_sent = []

    def send_part(h):
        arrived(shrunk_sent[h])
        total = shrunk[me["by"], h]
        for d in range(1, ny):
            total = total + shrunk_in[d - 1, h]
        reduced = split(total)
        group = []
        for d in range(1, nx + 1):
            to = peer("bx", d)
            rows = core_rows_ref[pl.ds(pl.multiple_of(to * tall, tall), tall), :]
            part[d - 1, h] = dot3(split(rows), reduced, NN)
            if d < nx:
                group.append(send("bx", d, part.at[d - 1, h], part_in.at[d - 1, h]))
        part_sent.append(group)

    send_part(0)

    arrived(col_a_sent)
    total = col_a[me["bz"]]
    for d in range(1, nz):
        total = total + col_a_in[d - 1]
    col_b[...] = total
    odd, pair = lax.rem(me["bx"], 2), lax.div(me["bx"], 2)
    col_b_sent = send("bx", 1, col_b.at[1 - odd], col_b_in, to=2 * pair + 1 - odd)

    for h in range(1, chunks):
        send_part(h)

    loads[5].wait()
    by_col = dot3(slab, split(col_test_ref[...]), NN)
    plane_a[...] = jnp.sum(by_col * row_test, axis=0, keepdims=True)
    plane_a_sent = send_all("by", lambda d: plane_a, lambda n: plane_a_in.at[n])
    terms = (by_col * plane_test).T
    block = row_a.shape[2]
    for y in range(ny):
        for z in range(nz):
            first = (y * nz + z) * block
            row_a[z, y] = terms[first:first + block, :]
    row_a_sent = send_all("bz", lambda d: row_a.at[peer("bz", d)], lambda n: row_a_in.at[n])

    half = nx // 2
    col_b_sent.wait_recv()
    col_c[...] = col_b[odd] + col_b_in[...]
    col_c_sent = []
    for d in range(1, half):
        to = lax.rem(pair + d, half)
        col_c_sent.append(send("bx", d, col_c.at[to], col_c_in.at[d - 1], to=2 * to + odd))

    arrived(plane_a_sent)
    total = plane_a[...]
    for d in range(1, ny):
        total = total + plane_a_in[d - 1]
    plane_b[...] = total
    plane_b_sent = send_all("bx", lambda d: plane_b, lambda n: plane_b_in.at[n])

    arrived(row_a_sent)
    total = row_a[me["bz"]]
    for d in range(1, nz):
        total = total + row_a_in[d - 1]
    row_b[...] = total
    row_b_sent = send_all("by", lambda d: row_b.at[peer("by", d)], lambda n: row_b_in.at[n])

    def finish_part(h):
        total = part[nx - 1, h]
        for d in range(1, nx):
            part_sent[h][d - 1].wait_recv()
            total = total + part_in[d - 1, h]
        full[h] = total
        gathered_ref[me["bz"], :, h * wide:(h + 1) * wide] = total
        return send_all("bz", lambda d: full.at[h], lambda n: full_in.at[n, h])

    full_sent = [finish_part(0)]

    arrived(row_b_sent)
    total = row_b[me["by"]]
    for d in range(1, ny):
        total = total + row_b_in[d - 1]
    row_ref[...] = total

    arrived(col_c_sent)
    total = col_c[pair]
    for d in range(1, half):
        total = total + col_c_in[d - 1]
    col_ref[...] = total

    for h in range(1, chunks):
        full_sent.append(finish_part(h))

    arrived(plane_b_sent)
    total = plane_b[...]
    for d in range(1, nx):
        total = total + plane_b_in[d - 1]
    plane_ref[...] = total

    for h in range(chunks):
        arrived(full_sent[h])
        for d in range(1, nz):
            gathered_ref[peer("bz", nz - d), :, h * wide:(h + 1) * wide] = full_in[d - 1, h]
    for copy in copies:
        copy.wait_send()


def core_kernel(
    planes_ref, gathered_ref, row_in, col_in, plane_in,
    row_ref, col_ref, plane_ref, out_ref,
    slots, out_sem, small_sem,
):
    count, rows = slots.shape[:2]
    steps = out_ref.shape[0] // rows
    small = [
        pltpu.make_async_copy(source, target, small_sem.at[n])
        for n, (source, target) in enumerate(
            ((row_in, row_ref), (col_in, col_ref), (plane_in, plane_ref))
        )
    ]

    def copy(step, slot):
        return pltpu.make_async_copy(
            slots.at[slot], out_ref.at[pl.ds(step * rows, rows)], out_sem.at[slot]
        )

    def body(step, _):
        slot = lax.rem(step, count)

        @pl.when(step >= count)
        def _():
            copy(step - count, slot).wait()

        for c in range(rows):
            row = step * rows + c
            value = planes_ref[0, row] * gathered_ref[0]
            for p in range(1, gathered_ref.shape[0]):
                value = value + planes_ref[p, row] * gathered_ref[p]
            slots[slot, c] = value
        copy(step, slot).start()
        return 0

    lax.fori_loop(0, steps, body, 0)
    for one in small:
        one.start()
    for step in range(steps - count, steps):
        copy(step, step % count).wait()
    for one in small:
        one.wait()


def on_device(nx, ny, nz, slab, plane_test, row_test, col_test, core_planes, core_rows, core_cols):
    rank = row_test.shape[1]
    ni, nj = slab.shape[1:]
    ab, bb = core_rows.shape[0] // nx, core_cols.shape[0] // ny
    rb, cb = rank // (ny * nz), rank // (nx * nz)
    chunks = 2 if bb % 256 == 0 else 1
    wide = bb // chunks
    shape = lambda *dims: jax.ShapeDtypeStruct(dims, F32)
    vmem = lambda *dims: pltpu.VMEM(dims, F32)
    inputs = (slab, plane_test, row_test, col_test, core_rows, core_cols)
    transfers = (2 + chunks) * (nz - 1) + (2 + chunks) * (ny - 1) + (1 + chunks) * (nx - 1) + nx // 2
    gathered, row_t, col_t, plane_sketch = pl.pallas_call(
        functools.partial(exchange_kernel, nx, ny, nz),
        out_shape=(shape(nz, ab, bb), shape(rb, ni), shape(cb, nj), shape(1, rank)),
        in_specs=[pl.BlockSpec(memory_space=pltpu.HBM)] * 6,
        out_specs=[pl.BlockSpec(memory_space=pltpu.VMEM)] * 4,
        scratch_shapes=[vmem(*a.shape) for a in inputs] + [
            vmem(ny, chunks, ni, wide), vmem(ny - 1, chunks, ni, wide),
            vmem(nx, chunks, ab, wide), vmem(nx - 1, chunks, ab, wide),
            vmem(chunks, ab, wide), vmem(nz - 1, chunks, ab, wide),
            vmem(nz, ny, rb, ni), vmem(nz - 1, ny, rb, ni),
            vmem(ny, rb, ni), vmem(ny - 1, rb, ni),
            vmem(nz, 2, nx // 2, cb, nj), vmem(nz - 1, 2, nx // 2, cb, nj),
            vmem(2, nx // 2, cb, nj), vmem(nx // 2, cb, nj),
            vmem(nx // 2, cb, nj), vmem(nx // 2 - 1, cb, nj),
            vmem(1, rank), vmem(ny - 1, 1, rank),
            vmem(1, rank), vmem(nx - 1, 1, rank),
            pltpu.SemaphoreType.DMA((transfers,)),
            pltpu.SemaphoreType.DMA((transfers,)),
            pltpu.SemaphoreType.DMA((len(inputs),)),
        ],
        compiler_params=pltpu.CompilerParams(
            collective_id=0, has_side_effects=True, vmem_limit_bytes=32 << 20
        ),
        name="exchange",
    )(*(pltpu.with_memory_space_constraint(a, pltpu.HBM) for a in inputs))
    depth = core_planes.shape[0]
    rows = min(depth, max(1, (1 << 17) // (ab * bb)))
    slots = min(8, depth // rows)
    row_t, col_t, plane_sketch, core_sketch = pl.pallas_call(
        core_kernel,
        out_shape=(shape(rb, ni), shape(cb, nj), shape(1, rank), shape(depth, ab, bb)),
        in_specs=[pl.BlockSpec(memory_space=pltpu.SMEM)]
        + [pl.BlockSpec(memory_space=pltpu.VMEM)] * 4,
        out_specs=[pl.BlockSpec(memory_space=pltpu.HBM)] * 4,
        scratch_shapes=[
            vmem(slots, rows, ab, bb),
            pltpu.SemaphoreType.DMA((slots,)),
            pltpu.SemaphoreType.DMA((3,)),
        ],
        compiler_params=pltpu.CompilerParams(vmem_limit_bytes=16 << 20),
        name="core",
    )(core_planes.T, gathered, row_t, col_t, plane_sketch)
    return plane_sketch, row_t.T, col_t.T, core_sketch


def solution(mesh):
    in_specs = (
        P(("groups", "bz"), "bx", "by"),
        P("bz", None),
        P("bx", None),
        P("by", None),
        P("bz", None),
        P(None, "bx"),
        P(None, "by"),
    )
    out_specs = (
        P(("groups", "bz"), None),
        P(("groups", "bx"), ("by", "bz")),
        P(("groups", "by"), ("bx", "bz")),
        P(("groups", "bz"), "bx", "by"),
    )
    sizes = [mesh.shape[name] for name in ("bx", "by", "bz")]
    return jax.shard_map(
        functools.partial(on_device, *sizes),
        mesh=mesh, in_specs=in_specs, out_specs=out_specs, check_vma=False,
    )
```
